128 devices in a mesh: cp: 4 (over y), ep: 32 (over x, z, core).
Axes of the slice: x: 4, y: 4, z: 4, core: 2. Of those that a mesh axis runs over, the one named last changes fastest.
Arguments:
- tokens: bfloat16 [32, 256, 3584], P('ep', 'cp'), may hold values from -6 to 6
- cotangent: bfloat16 [32, 256, 3584], P('ep', 'cp'), may hold values from -6 to 6
- routes: int32 [32, 256, 8], P('ep', 'cp'), may hold values from 0 to 127, all different within a row; in each aligned block of 64 rows (0 to 63, 64 to 127, ..., all dimensions but the last counted through in order) at most 5 rows name the same one
- router_weights: float32 [32, 256, 8], P('ep', 'cp'), may hold values from 0.02 to 0.5
- w_gate: bfloat16 [128, 3584, 1024], P(('cp', 'ep')), may hold values from -0.09375 to 0.09375
- w_up: bfloat16 [128, 3584, 1024], P(('cp', 'ep')), may hold values from -0.09375 to 0.09375
- w_down: bfloat16 [128, 1024, 3584], P(('cp', 'ep')), may hold values from -0.1875 to 0.1875
Outputs:
- layer_out: bfloat16 [32, 256, 3584], P('ep', 'cp')
- token_grad: bfloat16 [32, 256, 3584], P('ep', 'cp')
- gate_grad: float32 [32, 256, 8], P('ep', 'cp')
The draws below stay inside these ranges and needn't reach their ends.
Inputs may be any that keep to these rules, and one draw needn't show every extreme that they name: `routes`: each row names 8 distinct experts; in each aligned block of 64 rows (the rows of one device) no expert is named by more than 5 of the block's slots.
All inputs are finite; a program needn't handle non-finite values.
Results may differ from the reference program's by a relative error of at most 0.0058.
Values may be sent and summed in bfloat16 or wider, within the bound.
No kernel may reach another device: no remote copies, remote signals or barrier semaphores. Data moves between devices by JAX's collectives and lax.ppermute only.
A program may use at most 128 MiB of HBM per device.

```python
import math
import jax
import jax.numpy as jnp
import numpy as np
from jax import lax

D = 3584
FF = 1024
TOP = 8
SEQ_DEV = 64
LEN = 256
EXPERTS = 128
MOST = 5
N_EP = 32


def block_scale(own_key, extent, pieces, smallest, high):
    gain = 1.0
    for axis_at, parts in pieces:
        steps = jax.random.uniform(jax.random.fold_in(jax.random.fold_in(own_key, 6), axis_at), (parts,), jnp.float32, smallest / len(pieces), high / len(pieces))
        gain = gain * jnp.repeat(jnp.exp(steps), extent[axis_at] // parts).reshape((-1,) + (1,) * (len(extent) - 1 - axis_at))
    return gain


def shared_out(stream_key, own, number, rows, number_of, top, bound, lean):
    order = jax.random.permutation(stream_key, number_of)
    crowded, common = portions_of(number_of, rows * top, bound, lean, True), portions_of(number_of, rows * top, bound, lean, False)
    places = jnp.arange(number_of)

    def named(lengths, rotation):
        used = int((lengths > 0).sum())
        fixed = max(1, used // 4)
        moved = fixed + (places - fixed + rotation * (used - fixed)) % max(1, number_of - fixed)
        return jnp.zeros((number_of,), jnp.int32).at[order[jnp.where(places < fixed, places, moved)]].set(jnp.asarray(lengths, jnp.int32))

    lengths = jnp.where(number % 4 == 0, named(crowded, number // 4), named(common, number - number // 4 - 1))
    mixed = jax.random.permutation(jax.random.fold_in(own, 3), number_of)
    source_of, sink = mixed[0:number_of // 2 * 2:2], mixed[1:number_of // 2 * 2:2]
    room = jnp.minimum(lengths[source_of] - 1, bound - lengths[sink]) // 2
    room = jnp.where((source_of == order[0]) | (sink == order[0]) | (lengths[sink] == 0), 0, jnp.maximum(room, 0))
    moved = jax.random.randint(jax.random.fold_in(own, 4), (number_of // 2,), 0, 1 << 20) % (room + 1)
    lengths = lengths.at[source_of].add(-moved).at[sink].add(moved)
    members = jnp.searchsorted(jnp.cumsum(lengths), jnp.arange(rows * top), side="right").astype(jnp.int32)
    listing = members.reshape(top, rows).T
    listing = listing[jax.random.permutation(jax.random.fold_in(own, 1), rows)]
    rotation = jax.random.randint(jax.random.fold_in(own, 2), (rows, 1), 0, top)
    return jnp.take_along_axis(listing, (jnp.arange(top)[None, :] + rotation) % top, axis=1)


def portions_of(amount, total, limit, lean, full):
    portions = [(1 << 20) // math.isqrt(grade ** lean) + 1 for grade in range(1, amount + 1)]
    largest = limit if full else min(limit, max(-(-total // amount), total * portions[0] // sum(portions)))
    least = 1 if total - largest >= amount - 1 else 0
    given, surplus = [largest] + [least] * (amount - 1), total - largest - least * (amount - 1)
    while surplus > 0:
        free = [i for i in range(1, amount) if given[i] < largest] or [i for i in range(1, amount) if given[i] < limit]
        pool, left = sum([portions[i] for i in free]), surplus
        for i in free:
            extra = min(limit - given[i], max(1, left * portions[i] // pool), surplus)
            given[i] = given[i] + extra
            surplus = surplus - extra
    return np.array(given)


def bell_draw(stream_key, dims, deviation, limit, cuts=(), held_as=jnp.bfloat16):
    level = block_scale(stream_key, dims, cuts, -0.22, 0.18) if cuts else 1.0
    drawn = jax.random.normal(stream_key, dims, jnp.float32) * deviation * level
    return jnp.minimum(jnp.maximum(drawn, -limit), limit).astype(held_as)


def setup_inputs(seed: int = 0) -> dict:
    arg_keys = jax.random.split(jax.random.key(seed), 8)
    tokens = bell_draw(arg_keys[0], (N_EP, LEN, D), 1.0, 6.0, ((0, 32), (1, 4)))
    cotangent = bell_draw(arg_keys[1], (N_EP, LEN, D), 1.0, 6.0, ((0, 32), (1, 4)))
    routes_keys = jax.random.split(jax.random.fold_in(arg_keys[2], 1), N_EP * LEN // SEQ_DEV)
    routes_turns = jax.random.permutation(jax.random.fold_in(arg_keys[2], 3), N_EP * LEN // SEQ_DEV)
    routes = jax.vmap(lambda own, number: shared_out(jax.random.fold_in(arg_keys[2], 2), own, number, SEQ_DEV, EXPERTS, TOP, MOST, 2))(routes_keys, routes_turns).reshape((N_EP, LEN, TOP))
    router_weights = jnp.clip(jnp.exp(math.log(0.5) - 3.218876 * jax.random.uniform(arg_keys[3], (N_EP, LEN, TOP), jnp.float32) ** block_scale(arg_keys[3], (N_EP, LEN, TOP), ((0, 32), (1, 4)), -0.2, 0.2)), 0.02, 0.5)
    w_gate = bell_draw(arg_keys[4], (EXPERTS, D, FF), D ** -0.5, 0.09375, ((0, 128),))
    w_up = bell_draw(arg_keys[5], (EXPERTS, D, FF), D ** -0.5, 0.09375, ((0, 128),))
    w_down = bell_draw(arg_keys[6], (EXPERTS, FF, D), FF ** -0.5, 0.1875, ((0, 128),))
    return dict(tokens=tokens, cotangent=cotangent, routes=routes, router_weights=router_weights, w_gate=w_gate, w_up=w_up, w_down=w_down)


def expert_rows(inputs, grad_in, gate_matrix, up_matrix, down_matrix):
    gate_pre = jnp.dot(inputs, gate_matrix, preferred_element_type=jnp.float32)
    up_pre = jnp.dot(inputs, up_matrix, preferred_element_type=jnp.float32)
    sig_gate = jax.nn.sigmoid(gate_pre)
    silu_gate = gate_pre * sig_gate
    hidden = (silu_gate * up_pre).astype(jnp.bfloat16)
    expert_out = jnp.dot(hidden, down_matrix, preferred_element_type=jnp.float32).astype(jnp.bfloat16)
    grad_hidden = jnp.dot(grad_in, down_matrix.T, preferred_element_type=jnp.float32)
    grad_gate = (grad_hidden * up_pre * sig_gate * (1.0 + gate_pre * (1.0 - sig_gate))).astype(jnp.bfloat16)
    grad_up = (grad_hidden * silu_gate).astype(jnp.bfloat16)
    expert_grad = (jnp.dot(grad_gate, gate_matrix.T, preferred_element_type=jnp.float32)
                   + jnp.dot(grad_up, up_matrix.T, preferred_element_type=jnp.float32)).astype(jnp.bfloat16)
    return expert_out, expert_grad


def reference(tokens, cotangent, routes, router_weights, w_gate, w_up, w_down):
    total = N_EP * LEN
    padded_tokens = jnp.concatenate([tokens.reshape(total, D), jnp.zeros((1, D), jnp.bfloat16)], 0)
    padded_cot = jnp.concatenate([cotangent.reshape(total, D), jnp.zeros((1, D), jnp.bfloat16)], 0)
    flat_routes = routes.reshape(total * TOP)
    flat_mix = jnp.concatenate([router_weights.reshape(total * TOP), jnp.zeros((1,), jnp.float32)], 0)
    capacity = EXPERTS * MOST

    def visit(expert, carry):
        out_acc, grad_acc, gate_acc = carry
        slot_index = jnp.nonzero(flat_routes == expert, size=capacity, fill_value=total * TOP)[0].astype(jnp.int32)
        token_index = (slot_index // TOP).astype(jnp.int32)
        inputs = padded_tokens[token_index]
        grad_in = padded_cot[token_index]
        gate_matrix = lax.dynamic_index_in_dim(w_gate, expert, 0, keepdims=False)
        up_matrix = lax.dynamic_index_in_dim(w_up, expert, 0, keepdims=False)
        down_matrix = lax.dynamic_index_in_dim(w_down, expert, 0, keepdims=False)
        expert_out, expert_grad = expert_rows(inputs, grad_in, gate_matrix, up_matrix, down_matrix)
        mixing = flat_mix[slot_index]
        out_f = expert_out.astype(jnp.float32)
        out_acc = out_acc.at[token_index].add(mixing[:, None] * out_f)
        grad_acc = grad_acc.at[token_index].add(mixing[:, None] * expert_grad.astype(jnp.float32))
        gate_acc = gate_acc.at[slot_index].add(jnp.sum(grad_in.astype(jnp.float32) * out_f, -1))
        return out_acc, grad_acc, gate_acc

    start = (jnp.zeros((total + 1, D), jnp.float32), jnp.zeros((total + 1, D), jnp.float32),
             jnp.zeros((total * TOP + 1,), jnp.float32))
    out_acc, grad_acc, gate_acc = lax.fori_loop(0, EXPERTS, visit, start)
    layer_out = out_acc[:total].astype(jnp.bfloat16).reshape(N_EP, LEN, D)
    token_grad = grad_acc[:total].astype(jnp.bfloat16).reshape(N_EP, LEN, D)
    gate_grad = gate_acc[:total * TOP].reshape(N_EP, LEN, TOP)
    return (layer_out, token_grad, gate_grad)
```

```python
import functools

import jax
import jax.numpy as jnp
from jax import lax
from jax.experimental import pallas as pl
from jax.experimental.pallas import tpu as pltpu
from jax.sharding import PartitionSpec as P

LANES = 128
GROUPS = ((0, 3), (3, 5))
AXES = ("cp", "ep")
F32 = jnp.float32
BF16 = jnp.bfloat16
ANY = pl.BlockSpec(memory_space=pl.ANY)
VMEM = pl.BlockSpec(memory_space=pltpu.VMEM)
SMEM = pl.BlockSpec(memory_space=pltpu.SMEM)


def pack_kernel(top_k, slots, tokens, cotangent, out, flat, records, sem):
    positions, features = tokens.shape
    cols = features // LANES
    height = 2 * cols
    for j in range(cols):
        lanes = slice(j * LANES, (j + 1) * LANES)
        flat[pl.ds(j, positions, stride=height), :] = tokens[:, lanes].astype(F32)
        flat[pl.ds(cols + j, positions, stride=height), :] = cotangent[:, lanes].astype(F32)
    records[0:positions] = flat[...].reshape(positions, height, LANES).astype(BF16)
    records[positions] = jnp.zeros((height, LANES), BF16)

    @pl.loop(0, out.shape[0], unroll=8)
    def _(r):
        pltpu.make_async_copy(records.at[slots[r] // top_k], out.at[r], sem).start()

    pltpu.make_async_copy(out, out, sem).wait()


def pack(slots, tokens, cotangent, top_k):
    positions, features = tokens.shape
    height = 2 * features // LANES
    rows = slots.shape[0]
    return pl.pallas_call(
        functools.partial(pack_kernel, top_k),
        out_shape=jax.ShapeDtypeStruct((rows, height, LANES), BF16),
        in_specs=[SMEM, VMEM, VMEM],
        out_specs=ANY,
        scratch_shapes=[
            pltpu.VMEM((positions * height, LANES), F32),
            pltpu.VMEM((positions + 1, height, LANES), BF16),
            pltpu.SemaphoreType.DMA,
        ],
        cost_estimate=pl.CostEstimate(
            flops=0, transcendentals=0, bytes_accessed=rows * height * LANES * 4
        ),
        name="pack",
    )(slots, tokens, cotangent)


NT = (((1,), (1,)), ((), ()))


def expert_kernel(
    rec_in, w_gate, w_up, w_down, rec_out,
    rec, wg, wu, wd, inputs, grads, hidden, grad_gate, grad_up, flat, sems,
):
    rows, height, _ = rec.shape
    features, width = wg.shape
    cols = height // 2
    copies = [
        pltpu.make_async_copy(src, dst, sems.at[i])
        for i, (src, dst) in enumerate(
            ((rec_in, rec), (w_gate, wg), (w_up, wu), (w_down, wd))
        )
    ]
    for c in copies:
        c.start()
    copies[0].wait()
    step = 64

    @pl.loop(0, rows // step)
    def _(c):
        first = pl.multiple_of(c * step, step)
        part = flat.at[pl.ds(0, step * height)]
        part[...] = rec[pl.ds(first, step)].astype(F32).reshape(step * height, LANES)
        for j in range(cols):
            lanes = slice(j * LANES, (j + 1) * LANES)
            inputs[pl.ds(first, step), lanes] = part[pl.ds(j, step, stride=height), :].astype(BF16)
            grads[pl.ds(first, step), lanes] = part[
                pl.ds(cols + j, step, stride=height), :
            ].astype(BF16)

    for c in copies[1:]:
        c.wait()
    block = 256
    for h in range(width // block):
        part = slice(h * block, (h + 1) * block)
        gate_pre = jnp.dot(inputs[...], wg[:, part], preferred_element_type=F32)
        up_pre = jnp.dot(inputs[...], wu[:, part], preferred_element_type=F32)
        grad_hidden = lax.dot_general(grads[...], wd[part, :], NT, preferred_element_type=F32)
        sig = jax.nn.sigmoid(gate_pre)
        silu = gate_pre * sig
        hidden[:, part] = (silu * up_pre).astype(BF16)
        grad_gate[:, part] = (grad_hidden * up_pre * sig * (1.0 + gate_pre * (1.0 - sig))).astype(BF16)
        grad_up[:, part] = (grad_hidden * silu).astype(BF16)
    for h in range(features // block):
        part = slice(h * block, (h + 1) * block)
        expert_out = jnp.dot(hidden[...], wd[:, part], preferred_element_type=F32)
        expert_grad = lax.dot_general(
            grad_gate[...], wg[part, :], NT, preferred_element_type=F32
        ) + lax.dot_general(grad_up[...], wu[part, :], NT, preferred_element_type=F32)
        for j in range(block // LANES):
            at = h * (block // LANES) + j
            lanes = slice(j * LANES, (j + 1) * LANES)
            flat[pl.ds(at, rows, stride=height), :] = expert_out[:, lanes]
            flat[pl.ds(cols + at, rows, stride=height), :] = expert_grad[:, lanes]

    @pl.loop(0, rows // step)
    def _(c):
        first = pl.multiple_of(c * step, step)
        source = flat[pl.ds(pl.multiple_of(first * height, step * height), step * height), :]
        rec[pl.ds(first, step)] = source.reshape(step, height, LANES).astype(BF16)
        pltpu.make_async_copy(
            rec.at[pl.ds(first, step)], rec_out.at[pl.ds(first, step)], sems.at[0]
        ).start()

    pltpu.make_async_copy(rec, rec_out, sems.at[0]).wait()


def expert(records, w_gate, w_up, w_down):
    rows, height, _ = records.shape
    features, width = w_gate.shape
    return pl.pallas_call(
        expert_kernel,
        out_shape=jax.ShapeDtypeStruct(records.shape, BF16),
        in_specs=[ANY] * 4,
        out_specs=ANY,
        scratch_shapes=[
            pltpu.VMEM((rows, height, LANES), BF16),
            pltpu.VMEM((features, width), BF16),
            pltpu.VMEM((features, width), BF16),
            pltpu.VMEM((width, features), BF16),
            pltpu.VMEM((rows, features), BF16),
            pltpu.VMEM((rows, features), BF16),
            pltpu.VMEM((rows, width), BF16),
            pltpu.VMEM((rows, width), BF16),
            pltpu.VMEM((rows, width), BF16),
            pltpu.VMEM((rows * height, LANES), F32),
            pltpu.SemaphoreType.DMA((4,)),
        ],
        cost_estimate=pl.CostEstimate(
            flops=12 * rows * features * width,
            transcendentals=rows * width,
            bytes_accessed=6 * features * width + 4 * rows * height * LANES,
        ),
        compiler_params=pltpu.CompilerParams(vmem_limit_bytes=60 * 1024 * 1024),
        name="expert",
    )(records, w_gate, w_up, w_down)


def unpack_kernel(
    first, last, top_k, slots, weights, rec_in, cotangent, acc_in, dots_in, *rest
):
    if last:
        layer_out, token_grad, gate_grad, rec, acc, dots, cot, sems = rest
    else:
        acc, dots, rec, cot, sems = rest
    positions, features = cotangent.shape
    rows, height, _ = rec.shape
    cols = features // LANES
    load = pltpu.make_async_copy(rec_in, rec, sems.at[0])
    load.start()
    for j in range(cols):
        cot[pl.ds(j, positions, stride=cols), :] = cotangent[:, j * LANES : (j + 1) * LANES].astype(F32)
    if first:
        acc[...] = jnp.zeros_like(acc)
        dots[...] = jnp.zeros_like(dots)
    else:
        acc[...] = acc_in[...]
        dots[...] = dots_in[...]
    load.wait()

    @pl.loop(0, rows)
    def _(r):
        slot = slots[r]

        @pl.when(slot < positions * top_k)
        def _():
            token = slot // top_k
            value = rec[r].astype(F32)
            acc[token] += weights[slot] * value
            at = pl.multiple_of(token * cols, 4)
            product = cot[pl.ds(at, cols), :] * value[:cols]
            dots[pl.ds(slot, 1), :] = jnp.sum(product, axis=0, keepdims=True)

    if last:
        lane = lax.broadcasted_iota(jnp.int32, (positions, top_k), 1)
        grads = jnp.zeros((positions, top_k), F32)
        for k in range(top_k):
            column = jnp.sum(dots[pl.ds(k, positions, stride=top_k), :], axis=1, keepdims=True)
            grads = jnp.where(lane == k, column, grads)
        gate_grad[...] = grads
        flat = acc.reshape((positions + 1) * height, LANES)
        for j in range(cols):
            lanes = slice(j * LANES, (j + 1) * LANES)
            layer_out[:, lanes] = flat[pl.ds(j, positions, stride=height), :].astype(BF16)
            token_grad[:, lanes] = flat[pl.ds(cols + j, positions, stride=height), :].astype(BF16)


def unpack(slots, weights, records, cotangent, carry, last, top_k):
    positions, features = cotangent.shape
    rows, height, _ = records.shape
    acc_shape = (positions + 1, height, LANES)
    dots_shape = (positions * top_k, LANES)
    first = carry is None
    if first:
        carry = (jnp.zeros((8, LANES), F32), jnp.zeros((8, LANES), F32))
    scratch = [
        pltpu.VMEM((rows, height, LANES), BF16),
        pltpu.VMEM((positions * features // LANES, LANES), F32),
        pltpu.SemaphoreType.DMA((1,)),
    ]
    if last:
        out_shape = (
            jax.ShapeDtypeStruct((positions, features), BF16),
            jax.ShapeDtypeStruct((positions, features), BF16),
            jax.ShapeDtypeStruct((positions, top_k), F32),
        )
        scratch[1:1] = [pltpu.VMEM(acc_shape, F32), pltpu.VMEM(dots_shape, F32)]
    else:
        out_shape = (
            jax.ShapeDtypeStruct(acc_shape, F32),
            jax.ShapeDtypeStruct(dots_shape, F32),
        )
    return pl.pallas_call(
        functools.partial(unpack_kernel, first, last, top_k),
        out_shape=out_shape,
        in_specs=[SMEM, SMEM, ANY, VMEM, VMEM, VMEM],
        out_specs=tuple(VMEM for _ in out_shape),
        scratch_shapes=scratch,
        cost_estimate=pl.CostEstimate(
            flops=8 * rows * height * LANES,
            transcendentals=0,
            bytes_accessed=rows * height * LANES * 4,
        ),
        name="unpack",
    )(slots, weights, records, cotangent, *carry)


def exchange(value):
    return lax.all_to_all(value, AXES, split_axis=0, concat_axis=0, tiled=True)


def per_device(tokens, cotangent, routes, router_weights, w_gate, w_up, w_down):
    owners = lax.axis_size("cp") * lax.axis_size("ep")
    positions = tokens.shape[1]
    top_k = routes.shape[2]
    count = positions * top_k
    capacity = count // owners * 5 // 4
    flat_routes = routes[0].reshape(count)
    index = jnp.arange(count, dtype=jnp.int32)
    earlier = (flat_routes[None, :] == flat_routes[:, None]) & (index[None, :] < index[:, None])
    rank = jnp.sum(earlier.astype(jnp.int32), axis=1)
    place = flat_routes * capacity + rank
    holds = place[None, :] == jnp.arange(owners * capacity, dtype=jnp.int32)[:, None]
    slot_of = count + jnp.sum(jnp.where(holds, index[None, :] - count, 0), axis=1)
    slot_of = slot_of.reshape(owners, capacity)
    weights = router_weights[0].reshape(count)

    slots = [slot_of[:, a:b].reshape(owners * (b - a)) for a, b in GROUPS]
    sent = [pack(s, tokens[0], cotangent[0], top_k) for s in slots]
    arrived = [exchange(s) for s in sent]
    done = [expert(a, w_gate[0], w_up[0], w_down[0]) for a in arrived]
    returned = [exchange(d) for d in done]
    carry = None
    for i, (s, r) in enumerate(zip(slots, returned)):
        carry = unpack(s, weights, r, cotangent[0], carry, i == len(GROUPS) - 1, top_k)
    layer_out, token_grad, gate_grad = carry
    return layer_out[None], token_grad[None], gate_grad[None]


def solution(mesh):
    in_specs = (
        P("ep", "cp", None),
        P("ep", "cp", None),
        P("ep", "cp", None),
        P("ep", "cp", None),
        P(("cp", "ep"), None, None),
        P(("cp", "ep"), None, None),
        P(("cp", "ep"), None, None),
    )
    out_specs = (P("ep", "cp", None), P("ep", "cp", None), P("ep", "cp", None))
    return jax.shard_map(
        per_device, mesh=mesh, in_specs=in_specs, out_specs=out_specs, check_vma=False
    )
```

```python
import functools

import jax
import jax.numpy as jnp
from jax import lax
from jax.experimental import pallas as pl
from jax.experimental.pallas import tpu as pltpu
from jax.sharding import PartitionSpec as P

LANES = 128
GROUPS = ((0, 3), (3, 5))
AXES = ("cp", "ep")
SPAN = 128
EMPTY = 8 * SPAN + 64
F32 = jnp.float32
BF16 = jnp.bfloat16
ANY = pl.BlockSpec(memory_space=pl.ANY)
VMEM = pl.BlockSpec(memory_space=pltpu.VMEM)
SMEM = pl.BlockSpec(memory_space=pltpu.SMEM)


def route(routes, positions, owners):
    top_k = routes.shape[0]
    by_token = routes[...].astype(F32).T
    lane = lax.broadcasted_iota(jnp.int32, (positions, owners), 1).astype(F32)
    token = lax.broadcasted_iota(jnp.int32, (positions, owners), 0).astype(F32)
    named = jnp.zeros((positions, owners), F32)
    slot = token - EMPTY
    for k in range(top_k):
        match = by_token[:, k : k + 1] == lane
        named = jnp.where(match, 1.0, named)
        slot = jnp.where(match, slot + k * SPAN, slot)
    row = lax.broadcasted_iota(jnp.int32, (positions, positions), 0)
    col = lax.broadcasted_iota(jnp.int32, (positions, positions), 1)
    before = jnp.where(col < row, 1.0, 0.0).astype(BF16)
    rank = jnp.dot(before, named.astype(BF16), preferred_element_type=F32)
    rank = jnp.where(named > 0.0, rank, -1.0)
    rows = [
        jnp.sum(jnp.where(rank == float(i), slot, 0.0), axis=0, keepdims=True) + EMPTY
        for i in range(8)
    ]
    return jnp.concatenate(rows, axis=0).astype(jnp.int32)


def build_records(tokens, cotangent, flat, records):
    positions, features = tokens.shape
    cols = features // LANES
    height = 2 * cols
    for j in range(cols):
        lanes = slice(j * LANES, (j + 1) * LANES)
        flat[pl.ds(j, positions, stride=height), :] = tokens[:, lanes].astype(F32)
        flat[pl.ds(cols + j, positions, stride=height), :] = cotangent[:, lanes].astype(F32)
    records[0:positions] = flat[...].reshape(positions, height, LANES).astype(BF16)
    records[positions] = jnp.zeros((height, LANES), BF16)


def send_records(group, table, records, out, sem):
    first, last = group
    span = last - first

    @pl.loop(0, out.shape[0] // span, unroll=4)
    def _(e):
        for i in range(span):
            token = table[first + i, e] & (SPAN - 1)
            pltpu.make_async_copy(records.at[token], out.at[e * span + i], sem).start()

    pltpu.make_async_copy(out, out, sem).wait()


def first_pack_kernel(
    group, routes, tokens_in, cotangent_in, out, table_out,
    tokens, cotangent, table, table_smem, flat, records, sem, sems,
):
    positions = tokens.shape[0]
    load = [
        pltpu.make_async_copy(tokens_in, tokens, sems.at[0]),
        pltpu.make_async_copy(cotangent_in, cotangent, sems.at[1]),
    ]
    for c in load:
        c.start()
    table[...] = route(routes, positions, table.shape[1])
    keep = [
        pltpu.make_async_copy(table, table_smem, sems.at[2]),
        pltpu.make_async_copy(table, table_out, sems.at[3]),
    ]
    for c in keep:
        c.start()
    for c in load:
        c.wait()
    build_records(tokens, cotangent, flat, records)
    for c in keep:
        c.wait()
    send_records(group, table_smem, records, out, sem)


def next_pack_kernel(group, table, tokens, cotangent, out, flat, records, sem):
    build_records(tokens, cotangent, flat, records)
    send_records(group, table, records, out, sem)


def pack_cost(rows, height):
    return pl.CostEstimate(
        flops=0, transcendentals=0, bytes_accessed=rows * height * LANES * 4
    )


def first_pack(group, routes, tokens, cotangent, owners):
    positions, features = tokens.shape
    height = 2 * features // LANES
    rows = owners * (group[1] - group[0])
    return pl.pallas_call(
        functools.partial(first_pack_kernel, group),
        out_shape=(
            jax.ShapeDtypeStruct((rows, height, LANES), BF16),
            jax.ShapeDtypeStruct((8, owners), jnp.int32),
        ),
        in_specs=[VMEM, ANY, ANY],
        out_specs=(ANY, ANY),
        scratch_shapes=[
            pltpu.VMEM((positions, features), BF16),
            pltpu.VMEM((positions, features), BF16),
            pltpu.VMEM((8, owners), jnp.int32),
            pltpu.SMEM((8, owners), jnp.int32),
            pltpu.VMEM((positions * height, LANES), F32),
            pltpu.VMEM((positions + 1, height, LANES), BF16),
            pltpu.SemaphoreType.DMA,
            pltpu.SemaphoreType.DMA((4,)),
        ],
        cost_estimate=pack_cost(rows, height),
        name="first_pack",
    )(routes, tokens, cotangent)


def next_pack(group, table, tokens, cotangent):
    positions, features = tokens.shape
    height = 2 * features // LANES
    rows = table.shape[1] * (group[1] - group[0])
    return pl.pallas_call(
        functools.partial(next_pack_kernel, group),
        out_shape=jax.ShapeDtypeStruct((rows, height, LANES), BF16),
        in_specs=[SMEM, VMEM, VMEM],
        out_specs=ANY,
        scratch_shapes=[
            pltpu.VMEM((positions * height, LANES), F32),
            pltpu.VMEM((positions + 1, height, LANES), BF16),
            pltpu.SemaphoreType.DMA,
        ],
        cost_estimate=pack_cost(rows, height),
        name="next_pack",
    )(table, tokens, cotangent)


NT = (((1,), (1,)), ((), ()))


def expert_kernel(
    rec_in, w_gate, w_up, w_down, rec_out,
    rec, wg, wu, wd, inputs, grads, hidden, grad_gate, grad_up, flat, sems,
):
    rows, height, _ = rec.shape
    features, width = wg.shape
    cols = height // 2
    copies = [
        pltpu.make_async_copy(src, dst, sems.at[i])
        for i, (src, dst) in enumerate(
            ((rec_in, rec), (w_gate, wg), (w_up, wu), (w_down, wd))
        )
    ]
    for c in copies:
        c.start()
    copies[0].wait()
    step = 64

    @pl.loop(0, rows // step)
    def _(c):
        first = pl.multiple_of(c * step, step)
        part = flat.at[pl.ds(0, step * height)]
        part[...] = rec[pl.ds(first, step)].astype(F32).reshape(step * height, LANES)
        for j in range(cols):
            lanes = slice(j * LANES, (j + 1) * LANES)
            inputs[pl.ds(first, step), lanes] = part[pl.ds(j, step, stride=height), :].astype(BF16)
            grads[pl.ds(first, step), lanes] = part[
                pl.ds(cols + j, step, stride=height), :
            ].astype(BF16)

    for c in copies[1:]:
        c.wait()
    block = 256
    for h in range(width // block):
        part = slice(h * block, (h + 1) * block)
        gate_pre = jnp.dot(inputs[...], wg[:, part], preferred_element_type=F32)
        up_pre = jnp.dot(inputs[...], wu[:, part], preferred_element_type=F32)
        grad_hidden = lax.dot_general(grads[...], wd[part, :], NT, preferred_element_type=F32)
        sig = jax.nn.sigmoid(gate_pre)
        silu = gate_pre * sig
        hidden[:, part] = (silu * up_pre).astype(BF16)
        grad_gate[:, part] = (grad_hidden * up_pre * sig * (1.0 + gate_pre * (1.0 - sig))).astype(BF16)
        grad_up[:, part] = (grad_hidden * silu).astype(BF16)
    for h in range(features // block):
        part = slice(h * block, (h + 1) * block)
        expert_out = jnp.dot(hidden[...], wd[:, part], preferred_element_type=F32)
        expert_grad = lax.dot_general(
            grad_gate[...], wg[part, :], NT, preferred_element_type=F32
        ) + lax.dot_general(grad_up[...], wu[part, :], NT, preferred_element_type=F32)
        for j in range(block // LANES):
            at = h * (block // LANES) + j
            lanes = slice(j * LANES, (j + 1) * LANES)
            flat[pl.ds(at, rows, stride=height), :] = expert_out[:, lanes]
            flat[pl.ds(cols + at, rows, stride=height), :] = expert_grad[:, lanes]

    @pl.loop(0, rows // step)
    def _(c):
        first = pl.multiple_of(c * step, step)
        source = flat[pl.ds(pl.multiple_of(first * height, step * height), step * height), :]
        rec[pl.ds(first, step)] = source.reshape(step, height, LANES).astype(BF16)
        pltpu.make_async_copy(
            rec.at[pl.ds(first, step)], rec_out.at[pl.ds(first, step)], sems.at[0]
        ).start()

    pltpu.make_async_copy(rec, rec_out, sems.at[0]).wait()


def expert(records, w_gate, w_up, w_down):
    rows, height, _ = records.shape
    features, width = w_gate.shape
    return pl.pallas_call(
        expert_kernel,
        out_shape=jax.ShapeDtypeStruct(records.shape, BF16),
        in_specs=[ANY] * 4,
        out_specs=ANY,
        scratch_shapes=[
            pltpu.VMEM((rows, height, LANES), BF16),
            pltpu.VMEM((features, width), BF16),
            pltpu.VMEM((features, width), BF16),
            pltpu.VMEM((width, features), BF16),
            pltpu.VMEM((rows, features), BF16),
            pltpu.VMEM((rows, features), BF16),
            pltpu.VMEM((rows, width), BF16),
            pltpu.VMEM((rows, width), BF16),
            pltpu.VMEM((rows, width), BF16),
            pltpu.VMEM((rows * height, LANES), F32),
            pltpu.SemaphoreType.DMA((4,)),
        ],
        cost_estimate=pl.CostEstimate(
            flops=12 * rows * features * width,
            transcendentals=rows * width,
            bytes_accessed=6 * features * width + 4 * rows * height * LANES,
        ),
        compiler_params=pltpu.CompilerParams(vmem_limit_bytes=60 * 1024 * 1024),
        name="expert",
    )(records, w_gate, w_up, w_down)


def unpack_kernel(group, first, last, table, weights, rec_in, cotangent_in, *rest):
    if not first:
        acc_in, dots_in, *rest = rest
    if last:
        layer_out, token_grad, gate_grad, *rest = rest
    else:
        acc_out, dots_out, *rest = rest
    rec, cotangent, cot, acc, dots, sems = rest
    positions, features = cotangent.shape
    rows, height, _ = rec.shape
    top_k = weights.shape[0]
    cols = features // LANES
    chunks = sems.shape[0] - 3
    part = rows // chunks
    loads = [
        pltpu.make_async_copy(
            rec_in.at[pl.ds(c * part, part)], rec.at[pl.ds(c * part, part)], sems.at[3 + c]
        )
        for c in range(chunks)
    ]
    others = [pltpu.make_async_copy(cotangent_in, cotangent, sems.at[0])]
    if not first:
        others.append(pltpu.make_async_copy(acc_in, acc, sems.at[1]))
        others.append(pltpu.make_async_copy(dots_in, dots, sems.at[2]))
    for c in others[:1] + loads[:1] + others[1:] + loads[1:]:
        c.start()
    if first:
        acc[...] = jnp.zeros_like(acc)
        dots[...] = jnp.zeros_like(dots)
    cot[...] = jnp.zeros_like(cot)
    tall = cot.shape[1]
    flat_cot = cot.reshape(cot.shape[0] * tall, LANES)
    others[0].wait()
    for j in range(cols):
        flat_cot[pl.ds(j, positions, stride=tall), :] = cotangent[
            :, j * LANES : (j + 1) * LANES
        ].astype(F32)
    for c in others[1:]:
        c.wait()
    span = group[1] - group[0]
    together = 2 * span

    for c in range(chunks):
        loads[c].wait()

        @pl.loop(0, part // together)
        def _(step):
            todo = []
            for u in range(together):
                r = c * part + step * together + u
                expert_at = c * (part // span) + step * 2 + u // span
                slot = table[group[0] + u % span, expert_at]
                token = slot & (SPAN - 1)
                k = slot // SPAN
                weight = weights[k & (top_k - 1), token & (positions - 1)]
                value = rec[r].astype(F32)
                dot = jnp.sum(cot[token] * value[:tall], axis=0, keepdims=True)
                todo.append((token, k * positions + token, weight * value, dot))
            for token, at, scaled, dot in todo:
                acc[token] += scaled
                dots[pl.ds(at, 1), :] = dot

    if last:
        gate_grad[...] = jnp.sum(
            dots[0 : top_k * positions].reshape(top_k, positions, LANES), axis=2
        )
        flat = acc.reshape((positions + 1) * height, LANES)
        for j in range(cols):
            lanes = slice(j * LANES, (j + 1) * LANES)
            layer_out[:, lanes] = flat[pl.ds(j, positions, stride=height), :].astype(BF16)
            token_grad[:, lanes] = flat[pl.ds(cols + j, positions, stride=height), :].astype(BF16)
    else:
        stores = [
            pltpu.make_async_copy(acc, acc_out, sems.at[1]),
            pltpu.make_async_copy(dots, dots_out, sems.at[2]),
        ]
        for c in stores:
            c.start()
        for c in stores:
            c.wait()


def unpack(group, table, weights, records, cotangent, carry, last):
    positions, features = cotangent.shape
    rows, height, _ = records.shape
    top_k = weights.shape[0]
    cols = features // LANES
    acc_shape = (positions + 1, height, LANES)
    dots_shape = (top_k * positions + positions + 8, LANES)
    if last:
        out_shape = (
            jax.ShapeDtypeStruct((positions, features), BF16),
            jax.ShapeDtypeStruct((positions, features), BF16),
            jax.ShapeDtypeStruct((top_k, positions), F32),
        )
    else:
        out_shape = (
            jax.ShapeDtypeStruct(acc_shape, F32),
            jax.ShapeDtypeStruct(dots_shape, F32),
        )
    return pl.pallas_call(
        functools.partial(unpack_kernel, group, not carry, last),
        out_shape=out_shape,
        in_specs=[SMEM, SMEM, ANY, ANY] + [ANY] * len(carry),
        out_specs=tuple(VMEM if last else ANY for _ in out_shape),
        scratch_shapes=[
            pltpu.VMEM((rows, height, LANES), BF16),
            pltpu.VMEM((positions, features), BF16),
            pltpu.VMEM((positions + 1, -(-cols // 8) * 8, LANES), F32),
            pltpu.VMEM(acc_shape, F32),
            pltpu.VMEM(dots_shape, F32),
            pltpu.SemaphoreType.DMA((3 + 4,)),
        ],
        cost_estimate=pl.CostEstimate(
            flops=8 * rows * height * LANES,
            transcendentals=0,
            bytes_accessed=rows * height * LANES * 4,
        ),
        name="unpack",
    )(table, weights, records, cotangent, *carry)


def exchange(value):
    return lax.all_to_all(value, AXES, split_axis=0, concat_axis=0, tiled=True)


def per_device(tokens, cotangent, routes, router_weights, w_gate, w_up, w_down):
    owners = lax.axis_size("cp") * lax.axis_size("ep")
    tokens, cotangent = tokens[0], cotangent[0]
    routes, weights = routes[0].T, router_weights[0].T

    sent, table = first_pack(GROUPS[0], routes, tokens, cotangent, owners)
    sent = [sent] + [next_pack(g, table, tokens, cotangent) for g in GROUPS[1:]]
    arrived = [exchange(s) for s in sent]
    done = [expert(a, w_gate[0], w_up[0], w_down[0]) for a in arrived]
    returned = [exchange(d) for d in done]
    carry = ()
    for i, (g, r) in enumerate(zip(GROUPS, returned)):
        carry = unpack(g, table, weights, r, cotangent, carry, i == len(GROUPS) - 1)
    layer_out, token_grad, gate_grad = carry
    return layer_out[None], token_grad[None], gate_grad.T[None]


def solution(mesh):
    in_specs = (
        P("ep", "cp", None),
        P("ep", "cp", None),
        P("ep", "cp", None),
        P("ep", "cp", None),
        P(("cp", "ep"), None, None),
        P(("cp", "ep"), None, None),
        P(("cp", "ep"), None, None),
    )
    out_specs = (P("ep", "cp", None), P("ep", "cp", None), P("ep", "cp", None))
    return jax.shard_map(
        per_device, mesh=mesh, in_specs=in_specs, out_specs=out_specs, check_vma=False
    )
```

```python
import functools

import jax
import jax.numpy as jnp
from jax import lax
from jax.experimental import pallas as pl
from jax.experimental.pallas import tpu as pltpu
from jax.sharding import PartitionSpec as P

LANES = 128
CHUNKS = 8
UNROLL = 2
GROUPS = ((0, 3), (3, 5))
AXES = ("cp", "ep")
SPAN = 128
EMPTY = 8 * SPAN + 64
F32 = jnp.float32
BF16 = jnp.bfloat16
ANY = pl.BlockSpec(memory_space=pl.ANY)
VMEM = pl.BlockSpec(memory_space=pltpu.VMEM)
SMEM = pl.BlockSpec(memory_space=pltpu.SMEM)


def route(routes, positions, owners):
    top_k = routes.shape[0]
    by_token = routes[...].astype(F32).T
    lane = lax.broadcasted_iota(jnp.int32, (positions, owners), 1).astype(F32)
    token = lax.broadcasted_iota(jnp.int32, (positions, owners), 0).astype(F32)
    named = jnp.zeros((positions, owners), F32)
    slot = token - EMPTY
    for k in range(top_k):
        match = by_token[:, k : k + 1] == lane
        named = jnp.where(match, 1.0, named)
        slot = jnp.where(match, slot + k * SPAN, slot)
    row = lax.broadcasted_iota(jnp.int32, (positions, positions), 0)
    col = lax.broadcasted_iota(jnp.int32, (positions, positions), 1)
    before = jnp.where(col < row, 1.0, 0.0).astype(BF16)
    rank = jnp.dot(before, named.astype(BF16), preferred_element_type=F32)
    rank = jnp.where(named > 0.0, rank, -1.0)
    rows = [
        jnp.sum(jnp.where(rank == float(i), slot, 0.0), axis=0, keepdims=True) + EMPTY
        for i in range(8)
    ]
    return jnp.concatenate(rows, axis=0).astype(jnp.int32)


def build_records(tokens, cotangent, flat, records):
    positions, features = tokens.shape
    cols = features // LANES
    height = 2 * cols
    for j in range(cols):
        lanes = slice(j * LANES, (j + 1) * LANES)
        flat[pl.ds(j, positions, stride=height), :] = tokens[:, lanes].astype(F32)
        flat[pl.ds(cols + j, positions, stride=height), :] = cotangent[:, lanes].astype(F32)
    records[0:positions] = flat[...].reshape(positions, height, LANES).astype(BF16)
    records[positions] = jnp.zeros((height, LANES), BF16)


def send_records(group, table, records, out, sem):
    first, last = group
    span = last - first

    @pl.loop(0, out.shape[0] // span, unroll=4)
    def _(e):
        for i in range(span):
            token = table[first + i, e] & (SPAN - 1)
            pltpu.make_async_copy(records.at[token], out.at[e * span + i], sem).start()

    pltpu.make_async_copy(out, out, sem).wait()


def first_pack_kernel(
    group, routes_in, tokens_in, cotangent_in, out, table_out,
    routes, tokens, cotangent, table, table_smem, flat, records, sem, sems,
):
    positions = tokens.shape[0]
    load = [
        pltpu.make_async_copy(src, dst, sems.at[i])
        for i, (src, dst) in enumerate(
            ((routes_in, routes), (tokens_in, tokens), (cotangent_in, cotangent))
        )
    ]
    for c in load:
        c.start()
    load[0].wait()
    table[...] = route(routes, positions, table.shape[1])
    keep = [
        pltpu.make_async_copy(table, table_smem, sems.at[3]),
        pltpu.make_async_copy(table, table_out, sems.at[4]),
    ]
    for c in keep:
        c.start()
    for c in load[1:]:
        c.wait()
    build_records(tokens, cotangent, flat, records)
    keep[0].wait()
    send_records(group, table_smem, records, out, sem)
    keep[1].wait()


def next_pack_kernel(group, table, tokens, cotangent, out, flat, records, sem):
    build_records(tokens, cotangent, flat, records)
    send_records(group, table, records, out, sem)


def pack_cost(rows, height):
    return pl.CostEstimate(
        flops=0, transcendentals=0, bytes_accessed=rows * height * LANES * 4
    )


def first_pack(group, routes, tokens, cotangent, owners):
    positions, features = tokens.shape
    height = 2 * features // LANES
    rows = owners * (group[1] - group[0])
    return pl.pallas_call(
        functools.partial(first_pack_kernel, group),
        out_shape=(
            jax.ShapeDtypeStruct((rows, height, LANES), BF16),
            jax.ShapeDtypeStruct((8, owners), jnp.int32),
        ),
        in_specs=[ANY, ANY, ANY],
        out_specs=(ANY, ANY),
        scratch_shapes=[
            pltpu.VMEM(routes.shape, jnp.int32),
            pltpu.VMEM((positions, features), BF16),
            pltpu.VMEM((positions, features), BF16),
            pltpu.VMEM((8, owners), jnp.int32),
            pltpu.SMEM((8, owners), jnp.int32),
            pltpu.VMEM((positions * height, LANES), F32),
            pltpu.VMEM((positions + 1, height, LANES), BF16),
            pltpu.SemaphoreType.DMA,
            pltpu.SemaphoreType.DMA((5,)),
        ],
        cost_estimate=pack_cost(rows, height),
        name="first_pack",
    )(routes, tokens, cotangent)


def next_pack(group, table, tokens, cotangent):
    positions, features = tokens.shape
    height = 2 * features // LANES
    rows = table.shape[1] * (group[1] - group[0])
    return pl.pallas_call(
        functools.partial(next_pack_kernel, group),
        out_shape=jax.ShapeDtypeStruct((rows, height, LANES), BF16),
        in_specs=[SMEM, VMEM, VMEM],
        out_specs=ANY,
        scratch_shapes=[
            pltpu.VMEM((positions * height, LANES), F32),
            pltpu.VMEM((positions + 1, height, LANES), BF16),
            pltpu.SemaphoreType.DMA,
        ],
        cost_estimate=pack_cost(rows, height),
        name="next_pack",
    )(table, tokens, cotangent)


NT = (((1,), (1,)), ((), ()))


def expert_kernel(
    rec_in, w_gate, w_up, w_down, rec_out,
    rec, wg, wu, wd, inputs, grads, hidden, grad_gate, grad_up, flat, sems,
):
    rows, height, _ = rec.shape
    features, width = wg.shape
    cols = height // 2
    copies = [
        pltpu.make_async_copy(src, dst, sems.at[i])
        for i, (src, dst) in enumerate(
            ((rec_in, rec), (w_gate, wg), (w_up, wu), (w_down, wd))
        )
    ]
    for c in copies:
        c.start()
    copies[0].wait()
    step = 64

    @pl.loop(0, rows // step)
    def _(c):
        first = pl.multiple_of(c * step, step)
        part = flat.at[pl.ds(0, step * height)]
        part[...] = rec[pl.ds(first, step)].astype(F32).reshape(step * height, LANES)
        for j in range(cols):
            lanes = slice(j * LANES, (j + 1) * LANES)
            inputs[pl.ds(first, step), lanes] = part[pl.ds(j, step, stride=height), :].astype(BF16)
            grads[pl.ds(first, step), lanes] = part[
                pl.ds(cols + j, step, stride=height), :
            ].astype(BF16)

    for c in copies[1:]:
        c.wait()
    block = 256
    for h in range(width // block):
        part = slice(h * block, (h + 1) * block)
        gate_pre = jnp.dot(inputs[...], wg[:, part], preferred_element_type=F32)
        up_pre = jnp.dot(inputs[...], wu[:, part], preferred_element_type=F32)
        grad_hidden = lax.dot_general(grads[...], wd[part, :], NT, preferred_element_type=F32)
        sig = jax.nn.sigmoid(gate_pre)
        silu = gate_pre * sig
        hidden[:, part] = (silu * up_pre).astype(BF16)
        grad_gate[:, part] = (grad_hidden * up_pre * sig * (1.0 + gate_pre * (1.0 - sig))).astype(BF16)
        grad_up[:, part] = (grad_hidden * silu).astype(BF16)
    for h in range(features // block):
        part = slice(h * block, (h + 1) * block)
        expert_out = jnp.dot(hidden[...], wd[:, part], preferred_element_type=F32)
        expert_grad = lax.dot_general(
            grad_gate[...], wg[part, :], NT, preferred_element_type=F32
        ) + lax.dot_general(grad_up[...], wu[part, :], NT, preferred_element_type=F32)
        for j in range(block // LANES):
            at = h * (block // LANES) + j
            lanes = slice(j * LANES, (j + 1) * LANES)
            flat[pl.ds(at, rows, stride=height), :] = expert_out[:, lanes]
            flat[pl.ds(cols + at, rows, stride=height), :] = expert_grad[:, lanes]

    @pl.loop(0, rows // step)
    def _(c):
        first = pl.multiple_of(c * step, step)
        source = flat[pl.ds(pl.multiple_of(first * height, step * height), step * height), :]
        rec[pl.ds(first, step)] = source.reshape(step, height, LANES).astype(BF16)
        pltpu.make_async_copy(
            rec.at[pl.ds(first, step)], rec_out.at[pl.ds(first, step)], sems.at[0]
        ).start()

    pltpu.make_async_copy(rec, rec_out, sems.at[0]).wait()


def expert(records, w_gate, w_up, w_down):
    rows, height, _ = records.shape
    features, width = w_gate.shape
    return pl.pallas_call(
        expert_kernel,
        out_shape=jax.ShapeDtypeStruct(records.shape, BF16),
        in_specs=[ANY] * 4,
        out_specs=ANY,
        scratch_shapes=[
            pltpu.VMEM((rows, height, LANES), BF16),
            pltpu.VMEM((features, width), BF16),
            pltpu.VMEM((features, width), BF16),
            pltpu.VMEM((width, features), BF16),
            pltpu.VMEM((rows, features), BF16),
            pltpu.VMEM((rows, features), BF16),
            pltpu.VMEM((rows, width), BF16),
            pltpu.VMEM((rows, width), BF16),
            pltpu.VMEM((rows, width), BF16),
            pltpu.VMEM((rows * height, LANES), F32),
            pltpu.SemaphoreType.DMA((4,)),
        ],
        cost_estimate=pl.CostEstimate(
            flops=12 * rows * features * width,
            transcendentals=rows * width,
            bytes_accessed=6 * features * width + 4 * rows * height * LANES,
        ),
        compiler_params=pltpu.CompilerParams(vmem_limit_bytes=60 * 1024 * 1024),
        name="expert",
    )(records, w_gate, w_up, w_down)


def unpack_kernel(group, first, last, table_in, weights_in, rec_in, cotangent_in, *rest):
    if not first:
        acc_in, dots_in, cot_in, *rest = rest
    if last:
        layer_to, grad_to, gate_to, *rest = rest
    else:
        acc_out, dots_out, cot_out, *rest = rest
    (
        table, weights, rec, cotangent, cot, dots, sems, layer_out, token_grad, gate_grad, old_dots, *accs
    ) = rest
    acc = accs[0]
    positions, features = cotangent.shape
    rows, height, _ = rec.shape
    top_k = weights.shape[0]
    cols = features // LANES
    chunks = sems.shape[0] - 5
    part = rows // chunks
    loads = [
        pltpu.make_async_copy(
            rec_in.at[pl.ds(c * part, part)], rec.at[pl.ds(c * part, part)], sems.at[5 + c]
        )
        for c in range(chunks)
    ]
    tall = cot.shape[1]
    if first:
        others = [pltpu.make_async_copy(cotangent_in, cotangent, sems.at[0])]
    else:
        others = [
            pltpu.make_async_copy(src, dst, sems.at[i])
            for i, (src, dst) in enumerate(
                ((cot_in, cot), (acc_in, accs[1]), (dots_in, old_dots))
            )
        ]
    small = [
        pltpu.make_async_copy(table_in, table, sems.at[3]),
        pltpu.make_async_copy(weights_in, weights, sems.at[4]),
    ]
    for c in small + others[:1] + loads + others[1:]:
        c.start()
    acc[...] = jnp.zeros_like(acc)
    dots[...] = jnp.zeros_like(dots)
    if first:
        cot[...] = jnp.zeros_like(cot)
        flat_cot = cot.reshape(cot.shape[0] * tall, LANES)
        others[0].wait()
        for j in range(cols):
            flat_cot[pl.ds(j, positions, stride=tall), :] = cotangent[
                :, j * LANES : (j + 1) * LANES
            ].astype(F32)
    else:
        others[0].wait()
    for c in small:
        c.wait()
    span = group[1] - group[0]
    experts = UNROLL
    together = experts * span

    for c in range(chunks):
        loads[c].wait()

        @pl.loop(0, part // together)
        def _(step):
            todo = []
            for u in range(together):
                r = c * part + step * together + u
                expert_at = c * (part // span) + step * experts + u // span
                slot = table[group[0] + u % span, expert_at]
                token = slot & (SPAN - 1)
                k = slot // SPAN
                weight = weights[k & (top_k - 1), token & (positions - 1)]
                value = rec[r].astype(F32)
                dot = jnp.sum(cot[token] * value[:tall], axis=0, keepdims=True)
                todo.append((token, k * positions + token, weight * value, dot))
            for u, (token, at, scaled, dot) in enumerate(todo):
                acc[token] += scaled
                dots[pl.ds(at, 1), :] = dot

    if last:
        for c in others[1:]:
            c.wait()
        stores = [
            pltpu.make_async_copy(src, dst, sems.at[i])
            for i, (src, dst) in enumerate(
                ((layer_out, layer_to), (token_grad, grad_to), (gate_grad, gate_to))
            )
        ]
        flats = [a.reshape((positions + 1) * height, LANES) for a in accs]
        for at, out in enumerate((layer_out, token_grad)):
            for j in range(cols):
                rows_at = pl.ds(at * cols + j, positions, stride=height)
                total = sum((f[rows_at, :] for f in flats[1:]), flats[0][rows_at, :])
                out[:, j * LANES : (j + 1) * LANES] = total.astype(BF16)
            stores[at].start()
        both = dots[0 : top_k * positions] + old_dots[0 : top_k * positions]
        gate_grad[...] = jnp.sum(both.reshape(top_k, positions, LANES), axis=2)
        stores[2].start()
        for c in stores:
            c.wait()
    else:
        stores = [
            pltpu.make_async_copy(cot, cot_out, sems.at[0]),
            pltpu.make_async_copy(acc, acc_out, sems.at[1]),
            pltpu.make_async_copy(dots, dots_out, sems.at[2]),
        ]
        for c in stores:
            c.start()
        for c in stores:
            c.wait()


def unpack(group, table, weights, records, cotangent, carry, last):
    positions, features = cotangent.shape
    rows, height, _ = records.shape
    top_k = weights.shape[0]
    cols = features // LANES
    acc_shape = (positions + 1, height, LANES)
    cot_shape = (positions + 1, -(-cols // 8) * 8, LANES)
    dots_shape = (top_k * positions + positions + 8, LANES)
    if last:
        out_shape = (
            jax.ShapeDtypeStruct((positions, features), BF16),
            jax.ShapeDtypeStruct((positions, features), BF16),
            jax.ShapeDtypeStruct((top_k, positions), F32),
        )
    else:
        out_shape = (
            jax.ShapeDtypeStruct(acc_shape, F32),
            jax.ShapeDtypeStruct(dots_shape, F32),
            jax.ShapeDtypeStruct(cot_shape, F32),
        )
    return pl.pallas_call(
        functools.partial(unpack_kernel, group, not carry, last),
        out_shape=out_shape,
        in_specs=[ANY] * (4 + len(carry)),
        out_specs=tuple(ANY for _ in out_shape),
        scratch_shapes=[
            pltpu.SMEM(table.shape, jnp.int32),
            pltpu.SMEM(weights.shape, F32),
            pltpu.VMEM((rows, height, LANES), BF16),
            pltpu.VMEM((positions, features), BF16),
            pltpu.VMEM(cot_shape, F32),
            pltpu.VMEM(dots_shape, F32),
            pltpu.SemaphoreType.DMA((5 + CHUNKS,)),
            pltpu.VMEM((positions, features), BF16),
            pltpu.VMEM((positions, features), BF16),
            pltpu.VMEM((top_k, positions), F32),
            pltpu.VMEM(dots_shape, F32),
            pltpu.VMEM(acc_shape, F32),
        ]
        + [pltpu.VMEM(acc_shape, F32)] * bool(carry),
        cost_estimate=pl.CostEstimate(
            flops=8 * rows * height * LANES,
            transcendentals=0,
            bytes_accessed=rows * height * LANES * 4,
        ),
        name="unpack",
    )(table, weights, records, cotangent, *carry)


def exchange(value):
    return lax.all_to_all(value, AXES, split_axis=0, concat_axis=0, tiled=True)


def per_device(tokens, cotangent, routes, router_weights, w_gate, w_up, w_down):
    owners = lax.axis_size("cp") * lax.axis_size("ep")
    tokens, cotangent = tokens[0], cotangent[0]
    routes, weights = routes[0].T, router_weights[0].T

    sent, table = first_pack(GROUPS[0], routes, tokens, cotangent, owners)
    sent = [sent] + [next_pack(g, table, tokens, cotangent) for g in GROUPS[1:]]
    arrived = [exchange(s) for s in sent]
    done = [expert(a, w_gate[0], w_up[0], w_down[0]) for a in arrived]
    returned = [exchange(d) for d in done]
    carry = ()
    for i, (g, r) in enumerate(zip(GROUPS, returned)):
        carry = unpack(g, table, weights, r, cotangent, carry, i == len(GROUPS) - 1)
    layer_out, token_grad, gate_grad = carry
    return layer_out[None], token_grad[None], gate_grad.T[None]


def solution(mesh):
    in_specs = (
        P("ep", "cp", None),
        P("ep", "cp", None),
        P("ep", "cp", None),
        P("ep", "cp", None),
        P(("cp", "ep"), None, None),
        P(("cp", "ep"), None, None),
        P(("cp", "ep"), None, None),
    )
    out_specs = (P("ep", "cp", None), P("ep", "cp", None), P("ep", "cp", None))
    return jax.shard_map(
        per_device, mesh=mesh, in_specs=in_specs, out_specs=out_specs, check_vma=False
    )
```

```python
import functools

import jax
import jax.numpy as jnp
from jax import lax
from jax.experimental import pallas as pl
from jax.experimental.pallas import tpu as pltpu
from jax.sharding import PartitionSpec as P

LANES = 128
CHUNKS = 8
PIECES = 4
UNROLL = 2
GROUPS = ((0, 3), (3, 5))
AXES = ("cp", "ep")
SPAN = 128
EMPTY = 8 * SPAN + 64
F32 = jnp.float32
BF16 = jnp.bfloat16
ANY = pl.BlockSpec(memory_space=pl.ANY)
VMEM = pl.BlockSpec(memory_space=pltpu.VMEM)
SMEM = pl.BlockSpec(memory_space=pltpu.SMEM)


def route(routes, positions, owners):
    top_k = routes.shape[0]
    by_token = routes[...].astype(F32).T
    lane = lax.broadcasted_iota(jnp.int32, (positions, owners), 1).astype(F32)
    token = lax.broadcasted_iota(jnp.int32, (positions, owners), 0).astype(F32)
    named = jnp.zeros((positions, owners), F32)
    slot = token - EMPTY
    for k in range(top_k):
        match = by_token[:, k : k + 1] == lane
        named = jnp.where(match, 1.0, named)
        slot = jnp.where(match, slot + k * SPAN, slot)
    row = lax.broadcasted_iota(jnp.int32, (positions, positions), 0)
    col = lax.broadcasted_iota(jnp.int32, (positions, positions), 1)
    before = jnp.where(col < row, 1.0, 0.0).astype(BF16)
    rank = jnp.dot(before, named.astype(BF16), preferred_element_type=F32)
    rank = jnp.where(named > 0.0, rank, -1.0)
    rows = [
        jnp.sum(jnp.where(rank == float(i), slot, 0.0), axis=0, keepdims=True) + EMPTY
        for i in range(8)
    ]
    return jnp.concatenate(rows, axis=0).astype(jnp.int32)


def build_records(tokens, cotangent, flat, records):
    positions, features = tokens.shape
    cols = features // LANES
    height = 2 * cols
    for j in range(cols):
        lanes = slice(j * LANES, (j + 1) * LANES)
        flat[pl.ds(j, positions, stride=height), :] = tokens[:, lanes].astype(F32)
        flat[pl.ds(cols + j, positions, stride=height), :] = cotangent[:, lanes].astype(F32)
    records[0:positions] = flat[...].reshape(positions, height, LANES).astype(BF16)
    records[positions] = jnp.zeros((height, LANES), BF16)


def send_records(group, table, records, out, sem):
    first, last = group
    span = last - first

    @pl.loop(0, out.shape[0] // span, unroll=4)
    def _(e):
        for i in range(span):
            token = table[first + i, e] & (SPAN - 1)
            pltpu.make_async_copy(records.at[token], out.at[e * span + i], sem).start()

    pltpu.make_async_copy(out, out, sem).wait()


def first_pack_kernel(
    group, routes_in, tokens_in, cotangent_in, out, table_out,
    routes, tokens, cotangent, table, table_smem, flat, records, sem, sems,
):
    positions = tokens.shape[0]
    load = [
        pltpu.make_async_copy(src, dst, sems.at[i])
        for i, (src, dst) in enumerate(
            ((routes_in, routes), (tokens_in, tokens), (cotangent_in, cotangent))
        )
    ]
    for c in load:
        c.start()
    load[0].wait()
    table[...] = route(routes, positions, table.shape[1])
    keep = [
        pltpu.make_async_copy(table, table_smem, sems.at[3]),
        pltpu.make_async_copy(table, table_out, sems.at[4]),
    ]
    for c in keep:
        c.start()
    for c in load[1:]:
        c.wait()
    build_records(tokens, cotangent, flat, records)
    keep[0].wait()
    send_records(group, table_smem, records, out, sem)
    keep[1].wait()


def next_pack_kernel(group, table, tokens, cotangent, out, flat, records, sem):
    build_records(tokens, cotangent, flat, records)
    send_records(group, table, records, out, sem)


def pack_cost(rows, height):
    return pl.CostEstimate(
        flops=0, transcendentals=0, bytes_accessed=rows * height * LANES * 4
    )


def first_pack(group, routes, tokens, cotangent, owners):
    positions, features = tokens.shape
    height = 2 * features // LANES
    rows = owners * (group[1] - group[0])
    return pl.pallas_call(
        functools.partial(first_pack_kernel, group),
        out_shape=(
            jax.ShapeDtypeStruct((rows, height, LANES), BF16),
            jax.ShapeDtypeStruct((8, owners), jnp.int32),
        ),
        in_specs=[ANY, ANY, ANY],
        out_specs=(ANY, ANY),
        scratch_shapes=[
            pltpu.VMEM(routes.shape, jnp.int32),
            pltpu.VMEM((positions, features), BF16),
            pltpu.VMEM((positions, features), BF16),
            pltpu.VMEM((8, owners), jnp.int32),
            pltpu.SMEM((8, owners), jnp.int32),
            pltpu.VMEM((positions * height, LANES), F32),
            pltpu.VMEM((positions + 1, height, LANES), BF16),
            pltpu.SemaphoreType.DMA,
            pltpu.SemaphoreType.DMA((5,)),
        ],
        cost_estimate=pack_cost(rows, height),
        name="first_pack",
    )(routes, tokens, cotangent)


def next_pack(group, table, tokens, cotangent):
    positions, features = tokens.shape
    height = 2 * features // LANES
    rows = table.shape[1] * (group[1] - group[0])
    return pl.pallas_call(
        functools.partial(next_pack_kernel, group),
        out_shape=jax.ShapeDtypeStruct((rows, height, LANES), BF16),
        in_specs=[SMEM, VMEM, VMEM],
        out_specs=ANY,
        scratch_shapes=[
            pltpu.VMEM((positions * height, LANES), F32),
            pltpu.VMEM((positions + 1, height, LANES), BF16),
            pltpu.SemaphoreType.DMA,
        ],
        cost_estimate=pack_cost(rows, height),
        name="next_pack",
    )(table, tokens, cotangent)


NT = (((1,), (1,)), ((), ()))


def expert_kernel(
    rec_in, w_gate, w_up, w_down, rec_out,
    rec, wg, wu, wd, inputs, grads, hidden, grad_gate, grad_up, flat, sems,
):
    rows, height, _ = rec.shape
    features, width = wg.shape
    cols = height // 2
    copies = [
        pltpu.make_async_copy(src, dst, sems.at[i])
        for i, (src, dst) in enumerate(
            ((rec_in, rec), (w_gate, wg), (w_up, wu), (w_down, wd))
        )
    ]
    for c in copies:
        c.start()
    copies[0].wait()
    step = 64

    @pl.loop(0, rows // step)
    def _(c):
        first = pl.multiple_of(c * step, step)
        part = flat.at[pl.ds(0, step * height)]
        part[...] = rec[pl.ds(first, step)].astype(F32).reshape(step * height, LANES)
        for j in range(cols):
            lanes = slice(j * LANES, (j + 1) * LANES)
            inputs[pl.ds(first, step), lanes] = part[pl.ds(j, step, stride=height), :].astype(BF16)
            grads[pl.ds(first, step), lanes] = part[
                pl.ds(cols + j, step, stride=height), :
            ].astype(BF16)

    for c in copies[1:]:
        c.wait()
    block = 256
    for h in range(width // block):
        part = slice(h * block, (h + 1) * block)
        gate_pre = jnp.dot(inputs[...], wg[:, part], preferred_element_type=F32)
        up_pre = jnp.dot(inputs[...], wu[:, part], preferred_element_type=F32)
        grad_hidden = lax.dot_general(grads[...], wd[part, :], NT, preferred_element_type=F32)
        sig = jax.nn.sigmoid(gate_pre)
        silu = gate_pre * sig
        hidden[:, part] = (silu * up_pre).astype(BF16)
        grad_gate[:, part] = (grad_hidden * up_pre * sig * (1.0 + gate_pre * (1.0 - sig))).astype(BF16)
        grad_up[:, part] = (grad_hidden * silu).astype(BF16)
    for h in range(features // block):
        part = slice(h * block, (h + 1) * block)
        expert_out = jnp.dot(hidden[...], wd[:, part], preferred_element_type=F32)
        expert_grad = lax.dot_general(
            grad_gate[...], wg[part, :], NT, preferred_element_type=F32
        ) + lax.dot_general(grad_up[...], wu[part, :], NT, preferred_element_type=F32)
        for j in range(block // LANES):
            at = h * (block // LANES) + j
            lanes = slice(j * LANES, (j + 1) * LANES)
            flat[pl.ds(at, rows, stride=height), :] = expert_out[:, lanes]
            flat[pl.ds(cols + at, rows, stride=height), :] = expert_grad[:, lanes]

    @pl.loop(0, rows // step)
    def _(c):
        first = pl.multiple_of(c * step, step)
        source = flat[pl.ds(pl.multiple_of(first * height, step * height), step * height), :]
        rec[pl.ds(first, step)] = source.reshape(step, height, LANES).astype(BF16)
        pltpu.make_async_copy(
            rec.at[pl.ds(first, step)], rec_out.at[pl.ds(first, step)], sems.at[0]
        ).start()

    pltpu.make_async_copy(rec, rec_out, sems.at[0]).wait()


def expert(records, w_gate, w_up, w_down):
    rows, height, _ = records.shape
    features, width = w_gate.shape
    return pl.pallas_call(
        expert_kernel,
        out_shape=jax.ShapeDtypeStruct(records.shape, BF16),
        in_specs=[ANY] * 4,
        out_specs=ANY,
        scratch_shapes=[
            pltpu.VMEM((rows, height, LANES), BF16),
            pltpu.VMEM((features, width), BF16),
            pltpu.VMEM((features, width), BF16),
            pltpu.VMEM((width, features), BF16),
            pltpu.VMEM((rows, features), BF16),
            pltpu.VMEM((rows, features), BF16),
            pltpu.VMEM((rows, width), BF16),
            pltpu.VMEM((rows, width), BF16),
            pltpu.VMEM((rows, width), BF16),
            pltpu.VMEM((rows * height, LANES), F32),
            pltpu.SemaphoreType.DMA((4,)),
        ],
        cost_estimate=pl.CostEstimate(
            flops=12 * rows * features * width,
            transcendentals=rows * width,
            bytes_accessed=6 * features * width + 4 * rows * height * LANES,
        ),
        compiler_params=pltpu.CompilerParams(vmem_limit_bytes=60 * 1024 * 1024),
        name="expert",
    )(records, w_gate, w_up, w_down)


def unpack_kernel(group, first, last, table_in, weights_in, rec_in, cotangent_in, *rest):
    kept = 0 if first else 4
    carry_in, rest = rest[:kept], rest[kept:]
    sent = 3 if last else 4
    outs, rest = rest[:sent], rest[sent:]
    table, weights, rec, cotangent, cot, acc, dots, sems, *rest = rest
    results, old = rest[:3], rest[3:]
    positions, features = cotangent.shape
    rows, height, _ = rec.shape
    top_k = weights.shape[0]
    cols = features // LANES
    tall = cot.shape[1]
    part = rows // CHUNKS
    loads = [
        pltpu.make_async_copy(
            rec_in.at[pl.ds(c * part, part)], rec.at[pl.ds(c * part, part)], sems.at[6 + c]
        )
        for c in range(CHUNKS)
    ]
    if first:
        others = [pltpu.make_async_copy(cotangent_in, cotangent, sems.at[0])]
    else:
        others = [
            pltpu.make_async_copy(src, dst, sems.at[i])
            for i, (src, dst) in enumerate(zip(carry_in, (cot, *old)))
        ]
    small = [
        pltpu.make_async_copy(table_in, table, sems.at[4]),
        pltpu.make_async_copy(weights_in, weights, sems.at[5]),
    ]
    for c in small + others[:1] + loads + others[1:]:
        c.start()
    acc[...] = jnp.zeros_like(acc)
    dots[...] = jnp.zeros_like(dots)
    if first:
        cot[...] = jnp.zeros_like(cot)
        flat_cot = cot.reshape(cot.shape[0] * tall, LANES)
        others[0].wait()
        for j in range(cols):
            flat_cot[pl.ds(j, positions, stride=tall), :] = cotangent[
                :, j * LANES : (j + 1) * LANES
            ].astype(F32)
    else:
        others[0].wait()
    for c in small:
        c.wait()
    span = group[1] - group[0]
    together = UNROLL * span

    for c in range(CHUNKS):
        loads[c].wait()

        @pl.loop(0, part // together)
        def _(step):
            todo = []
            for u in range(together):
                r = c * part + step * together + u
                expert_at = c * (part // span) + step * UNROLL + u // span
                slot = table[group[0] + u % span, expert_at]
                token = slot & (SPAN - 1)
                k = slot // SPAN
                weight = weights[k & (top_k - 1), token & (positions - 1)]
                value = rec[r].astype(F32)
                dot = jnp.sum(cot[token] * value[:tall], axis=0, keepdims=True)
                todo.append((token, k * positions + token, weight * value, dot))
            for token, at, scaled, dot in todo:
                acc[token] += scaled
                dots[pl.ds(at, 1), :] = dot

    for c in others[1:]:
        c.wait()
    flat = acc.reshape((positions + 1) * height, LANES)
    piece = cols // PIECES
    stores = []
    for at in range(2):
        for p in range(PIECES):
            for j in range(p * piece, (p + 1) * piece):
                lanes = slice(j * LANES, (j + 1) * LANES)
                total = flat[pl.ds(at * cols + j, positions, stride=height), :]
                if not first:
                    total = total + old[at][:, lanes]
                results[at][:, lanes] = total.astype(results[at].dtype)
            lanes = pl.ds(p * piece * LANES, piece * LANES)
            store = pltpu.make_async_copy(
                results[at].at[:, lanes], outs[at + sent - 3].at[:, lanes], sems.at[6 + len(stores)]
            )
            store.start()
            stores.append(store)
    total = jnp.sum(dots[0 : top_k * positions].reshape(top_k, positions, LANES), axis=2)
    if not first:
        total = total + old[2][...]
    results[2][...] = total
    stores.append(pltpu.make_async_copy(results[2], outs[-1], sems.at[5]))
    stores[-1].start()
    if not last:
        stores.append(pltpu.make_async_copy(cot, outs[0], sems.at[4]))
        stores[-1].start()
    for c in stores:
        c.wait()


def unpack(group, table, weights, records, cotangent, carry, last):
    positions, features = cotangent.shape
    rows, height, _ = records.shape
    top_k = weights.shape[0]
    cols = features // LANES
    cot_shape = (positions + 1, -(-cols // 8) * 8, LANES)
    kind = BF16 if last else F32
    results = [
        ((positions, features), kind), ((positions, features), kind), ((top_k, positions), F32)
    ]
    sent = results if last else [(cot_shape, F32)] + results
    return pl.pallas_call(
        functools.partial(unpack_kernel, group, not carry, last),
        out_shape=tuple(jax.ShapeDtypeStruct(*r) for r in sent),
        in_specs=[ANY] * (4 + len(carry)),
        out_specs=tuple(ANY for _ in sent),
        scratch_shapes=[
            pltpu.SMEM(table.shape, jnp.int32),
            pltpu.SMEM(weights.shape, F32),
            pltpu.VMEM((rows, height, LANES), BF16),
            pltpu.VMEM((positions, features), BF16),
            pltpu.VMEM(cot_shape, F32),
            pltpu.VMEM((positions + 1, height, LANES), F32),
            pltpu.VMEM((top_k * positions + positions + 8, LANES), F32),
            pltpu.SemaphoreType.DMA((6 + CHUNKS,)),
        ]
        + [pltpu.VMEM(*r) for r in results]
        + [pltpu.VMEM(shape, F32) for shape, _ in results if carry],
        cost_estimate=pl.CostEstimate(
            flops=8 * rows * height * LANES,
            transcendentals=0,
            bytes_accessed=rows * height * LANES * 4,
        ),
        name="unpack",
    )(table, weights, records, cotangent, *carry)


def exchange(value):
    return lax.all_to_all(value, AXES, split_axis=0, concat_axis=0, tiled=True)


def per_device(tokens, cotangent, routes, router_weights, w_gate, w_up, w_down):
    owners = lax.axis_size("cp") * lax.axis_size("ep")
    tokens, cotangent = tokens[0], cotangent[0]
    routes, weights = routes[0].T, router_weights[0].T

    sent, table = first_pack(GROUPS[0], routes, tokens, cotangent, owners)
    sent = [sent] + [next_pack(g, table, tokens, cotangent) for g in GROUPS[1:]]
    arrived = [exchange(s) for s in sent]
    done = [expert(a, w_gate[0], w_up[0], w_down[0]) for a in arrived]
    returned = [exchange(d) for d in done]
    carry = ()
    for i, (g, r) in enumerate(zip(GROUPS, returned)):
        carry = unpack(g, table, weights, r, cotangent, carry, i == len(GROUPS) - 1)
    layer_out, token_grad, gate_grad = carry
    return layer_out[None], token_grad[None], gate_grad.T[None]


def solution(mesh):
    in_specs = (
        P("ep", "cp", None),
        P("ep", "cp", None),
        P("ep", "cp", None),
        P("ep", "cp", None),
        P(("cp", "ep"), None, None),
        P(("cp", "ep"), None, None),
        P(("cp", "ep"), None, None),
    )
    out_specs = (P("ep", "cp", None), P("ep", "cp", None), P("ep", "cp", None))
    return jax.shard_map(
        per_device, mesh=mesh, in_specs=in_specs, out_specs=out_specs, check_vma=False
    )
```
